32 devices in a mesh: row: 8 (over z, y), col: 4 (over x, core).
Axes of the slice: x: 2, y: 2, z: 4, core: 2. Of those that a mesh axis runs over, the one named last changes fastest.
Arguments:
- trail_adjoint: float32 [4096, 4096], P('row', 'col'), may hold values from -6 to 6
- lower_new: float32 [4096, 256], P('row', 'col'), may hold values from -0.09375 to 0.09375
- upper_new: float32 [256, 4096], P('row', 'col'), may hold values from -0.09375 to 0.09375
- lower_old_top: float32 [256, 256], replicated, may hold values from -0.375 to 0.375
- lower_old: float32 [4096, 256], P('row', 'col'), may hold values from -0.09375 to 0.09375
- upper_old_left: float32 [256, 256], replicated, may hold values from -0.375 to 0.375
- upper_old: float32 [256, 4096], P('row', 'col'), may hold values from -0.09375 to 0.09375
- diag_lower_new: float32 [256, 256], replicated, as said below
- diag_upper_new: float32 [256, 256], replicated, as said below
- inverse_lower_new: float32 [256, 256], replicated, as said below
- inverse_upper_new: float32 [256, 256], replicated, as said below
- diag_lower_old: float32 [256, 256], replicated, as said below
- diag_upper_old: float32 [256, 256], replicated, as said below
- inverse_lower_old: float32 [256, 256], replicated, as said below
- inverse_upper_old: float32 [256, 256], replicated, as said below
Outputs:
- corner_old: float32 [256, 256], replicated
- strip_top: float32 [256, 256], replicated
- strip_bottom: float32 [4096, 256], P(('row', 'col'))
- band_left: float32 [256, 256], replicated
- band_right: float32 [256, 4096], P(None, 'col')
The draws below stay inside these ranges and needn't reach their ends.
Inputs may be any that keep to these rules, and one draw needn't show every extreme that they name: `diag_lower_new`: unit lower triangular. `diag_upper_new`: upper triangular, diagonal from 1 to 2. `inverse_lower_new`: the inverse of diag_lower_new. `inverse_upper_new`: the inverse of diag_upper_new. `diag_lower_old`: unit lower triangular. `diag_upper_old`: upper triangular, diagonal from 1 to 2. `inverse_lower_old`: the inverse of diag_lower_old. `inverse_upper_old`: the inverse of diag_upper_old.
All inputs are finite; a program needn't handle non-finite values.
Results may differ from the reference program's by a relative error of at most 0.000075.
Values sent between devices are 32-bit elements; how exact they have to be, the bound alone decides.
A program may use at most 128 MiB of HBM per device.

```python
import math
import jax
import jax.numpy as jnp
from jax import lax

B = 256
M = 4096


def triangle_pair(key, marker, downward):
    folded = jax.random.fold_in(key, marker)
    seed_noise, seed_scale = jax.random.split(folded)
    noise = jax.random.normal(seed_noise, (B, B), jnp.float32) * (0.3 / math.sqrt(B))
    identity = jnp.eye(B, dtype=jnp.float32)
    if downward:
        factor = jnp.tril(noise, -1) + identity
    else:
        scales = jax.random.uniform(seed_scale, (B,), jnp.float32, 1.0, 2.0)
        factor = jnp.triu(noise, 1) + jnp.diag(scales)
    inverse = jax.scipy.linalg.solve_triangular(factor, identity, lower=downward)
    return (factor, inverse)


def draw_diag_lower_new(key, part):
    return triangle_pair(key, 1, True)[0]


def draw_inverse_lower_new(key, part):
    return triangle_pair(key, 1, True)[1]


def draw_diag_upper_new(key, part):
    return triangle_pair(key, 2, False)[0]


def draw_inverse_upper_new(key, part):
    return triangle_pair(key, 2, False)[1]


def draw_diag_lower_old(key, part):
    return triangle_pair(key, 3, True)[0]


def draw_inverse_lower_old(key, part):
    return triangle_pair(key, 3, True)[1]


def draw_diag_upper_old(key, part):
    return triangle_pair(key, 4, False)[0]


def draw_inverse_upper_old(key, part):
    return triangle_pair(key, 4, False)[1]


def raised(entries, rng, source, target, parts, factor):
    def block_of(axis_at):
        return (jnp.arange(entries.shape[axis_at]) // (entries.shape[axis_at] // parts)).reshape((-1,) + (1,) * (entries.ndim - 1 - axis_at))

    first = jax.random.permutation(rng, parts)[block_of(target)]
    second = (block_of(target) + parts // 2) % parts
    return jnp.where((block_of(source) == first) | (block_of(source) == second), factor * entries, entries)


def block_levels(stream_key, dims, pieces, low, largest):
    gain = 1.0
    for dim, shards_of in pieces:
        heights = jax.random.uniform(jax.random.fold_in(jax.random.fold_in(stream_key, 6), dim), (shards_of,), jnp.float32, low / len(pieces), largest / len(pieces))
        gain = gain * jnp.repeat(jnp.exp(heights), dims[dim] // shards_of).reshape((-1,) + (1,) * (len(dims) - 1 - dim))
    return gain


def gaussian(own_key, shape, scale, bound, pieces=(), held_as=jnp.bfloat16):
    drawn = scale * jax.random.normal(own_key, shape, jnp.float32)
    if pieces:
        drawn = drawn * block_levels(own_key, shape, pieces, -0.22, 0.18)
    return jnp.clip(drawn, -bound, bound).astype(held_as)


def noise_with(own_key, extent, spread, bound, shards, heavy, kind=jnp.bfloat16):
    drawn = spread * jax.random.normal(own_key, extent, jnp.float32)
    if shards:
        drawn = drawn * block_levels(own_key, extent, shards, -0.22, 0.18)
    return jnp.clip(raised(drawn, jax.random.fold_in(own_key, 3), *heavy), -bound, bound).astype(kind)


def setup_inputs(seed: int = 0) -> dict:
    streams_of = jax.random.split(jax.random.key(seed), 16)
    trail_adjoint = noise_with(streams_of[0], (M, M), 1.0, 6.0, ((0, 8), (1, 4)), (1, 0, 8, 2.0), jnp.float32)
    lower_new = gaussian(streams_of[1], (M, B), M ** -0.5, 0.09375, ((0, 8), (1, 4)), jnp.float32)
    upper_new = gaussian(streams_of[2], (B, M), M ** -0.5, 0.09375, ((0, 8), (1, 4)), jnp.float32)
    lower_old_top = gaussian(streams_of[3], (B, B), B ** -0.5, 0.375, (), jnp.float32)
    lower_old = gaussian(streams_of[4], (M, B), M ** -0.5, 0.09375, ((0, 8), (1, 4)), jnp.float32)
    upper_old_left = gaussian(streams_of[5], (B, B), B ** -0.5, 0.375, (), jnp.float32)
    upper_old = gaussian(streams_of[6], (B, M), M ** -0.5, 0.09375, ((0, 8), (1, 4)), jnp.float32)
    diag_lower_new = draw_diag_lower_new(jax.random.fold_in(streams_of[15], 71), 0)
    diag_upper_new = draw_diag_upper_new(jax.random.fold_in(streams_of[15], 71), 0)
    inverse_lower_new = draw_inverse_lower_new(jax.random.fold_in(streams_of[15], 71), 0)
    inverse_upper_new = draw_inverse_upper_new(jax.random.fold_in(streams_of[15], 71), 0)
    diag_lower_old = draw_diag_lower_old(jax.random.fold_in(streams_of[15], 71), 0)
    diag_upper_old = draw_diag_upper_old(jax.random.fold_in(streams_of[15], 71), 0)
    inverse_lower_old = draw_inverse_lower_old(jax.random.fold_in(streams_of[15], 71), 0)
    inverse_upper_old = draw_inverse_upper_old(jax.random.fold_in(streams_of[15], 71), 0)
    return dict(trail_adjoint=trail_adjoint, lower_new=lower_new, upper_new=upper_new, lower_old_top=lower_old_top, lower_old=lower_old, upper_old_left=upper_old_left, upper_old=upper_old, diag_lower_new=diag_lower_new, diag_upper_new=diag_upper_new, inverse_lower_new=inverse_lower_new, inverse_upper_new=inverse_upper_new, diag_lower_old=diag_lower_old, diag_upper_old=diag_upper_old, inverse_lower_old=inverse_lower_old, inverse_upper_old=inverse_upper_old)


precise = lax.Precision.HIGHEST

def product(left, right):
    return jnp.dot(left, right, precision=precise)

def diag_adjoint(lower_factor, upper_factor, lower_inverse, upper_inverse, lower_grad, upper_grad):
    inner = jnp.tril(product(lower_factor.T, lower_grad), -1) + jnp.triu(product(upper_grad, upper_factor.T))
    return product(product(lower_inverse.T, inner), upper_inverse.T)

def reference(trail_adjoint, lower_new, upper_new, lower_old_top, lower_old, upper_old_left, upper_old, diag_lower_new, diag_upper_new, inverse_lower_new, inverse_upper_new, diag_lower_old, diag_upper_old, inverse_lower_old, inverse_upper_old):
    lower_adj_new = -product(trail_adjoint, upper_new.T)
    upper_adj_new = -product(lower_new.T, trail_adjoint)
    strip_new = product(lower_adj_new, inverse_upper_new.T)
    band_new = product(inverse_lower_new.T, upper_adj_new)
    corner_new = diag_adjoint(diag_lower_new, diag_upper_new, inverse_lower_new, inverse_upper_new, -product(band_new, upper_new.T), -product(lower_new.T, strip_new))
    strip_top = product(-(product(corner_new, upper_old_left.T) + product(band_new, upper_old.T)), inverse_upper_old.T)
    strip_bottom = product(-(product(strip_new, upper_old_left.T) + product(trail_adjoint, upper_old.T)), inverse_upper_old.T)
    band_left = product(inverse_lower_old.T, -(product(lower_old_top.T, corner_new) + product(lower_old.T, strip_new)))
    band_right = product(inverse_lower_old.T, -(product(lower_old_top.T, band_new) + product(lower_old.T, trail_adjoint)))
    lower_grad = -(product(band_left, upper_old_left.T) + product(band_right, upper_old.T))
    upper_grad = -(product(lower_old_top.T, strip_top) + product(lower_old.T, strip_bottom))
    corner_old = diag_adjoint(diag_lower_old, diag_upper_old, inverse_lower_old, inverse_upper_old, lower_grad, upper_grad)
    return (corner_old, strip_top, strip_bottom, band_left, band_right)
```

```python
import jax
import jax.numpy as jnp
from jax import lax
from jax.sharding import PartitionSpec as P

precise = lax.Precision.HIGH


def dot(left, right, a, b):
    return lax.dot_general(left, right, (((a,), (b,)), ((), ())), precision=precise)


def body(an, ln, un, lot, lo, uol, uo, dln, dun, iln, iun, dlo, duo, ilo, iuo):
    width = iln.shape[0]
    uppers = lax.all_gather(jnp.concatenate((un[None], uo[None])), "row", axis=1, tiled=True)
    lowers = lax.all_gather(jnp.concatenate((ln[None], lo[None])), "col", axis=2, tiled=True)
    un, uo = uppers[0], uppers[1]
    ln, lo = lowers[0], lowers[1]
    mix_u = dot(dot(iuo, uol, 1, 0), iun, 1, 0)
    mix_l = dot(dot(iln, lot, 1, 0), ilo, 1, 0)
    ut = dot(iuo, uo, 1, 0) - dot(mix_u, un, 1, 0)
    lt = dot(lo, ilo, 1, 0) - dot(ln, mix_l, 1, 0)
    strip = -dot(an, ut, 1, 1)
    band = -dot(lt, an, 0, 0)
    left = -dot(band, un, 1, 1)
    both = -dot(jnp.concatenate((ln, lt), axis=1), strip, 0, 0)
    small = lax.psum(jnp.concatenate((left, both), axis=0), ("row", "col"))
    strip = lax.psum_scatter(strip, "col", scatter_dimension=0, tiled=True)
    band = lax.psum(band, "row")
    band_left = dot(small[:width], iun, 1, 1)
    strip_top = dot(iln, small[width : 2 * width], 0, 0)
    corner = small[2 * width :]
    return (corner, strip_top, strip, band_left, band)


def solution(mesh):
    split, whole = P("row", "col"), P()
    return jax.shard_map(
        body,
        mesh=mesh,
        in_specs=(split, split, split, whole, split, whole, split) + (whole,) * 8,
        out_specs=(P(), P(), P(("row", "col"), None), P(), P(None, "col")),
        check_vma=False,
    )
```

```python
import functools

import jax
import jax.numpy as jnp
from jax import lax
from jax.experimental import pallas as pl
from jax.experimental.pallas import tpu as pltpu
from jax.sharding import PartitionSpec as P

f32, bf16 = jnp.float32, jnp.bfloat16
NN, NT = ((1,), (0,)), ((1,), (1,))


def split(x):
    high = x.astype(bf16)
    return high, (x - high.astype(f32)).astype(bf16)


def mul(a, b, dims=NN):
    def one(x, y):
        return lax.dot_general(x, y, (dims, ((), ())), preferred_element_type=f32)

    return one(a[0], b[0]) + (one(a[0], b[1]) + one(a[1], b[0]))


def start(axis, n, me, source, target, send, recv):
    copies = []
    for d in range(1, n):
        peer = lax.rem(me + d, n)
        copy = pltpu.make_async_remote_copy(
            src_ref=source(peer),
            dst_ref=target,
            send_sem=send.at[d],
            recv_sem=recv.at[d],
            device_id={axis: peer},
            device_id_type=pl.DeviceIdType.MESH,
        )
        copy.start()
        copies.append(copy)
    return copies


def arrive(copies):
    for copy in copies:
        copy.wait_recv()


def kernel(
    nr, nc, a_hbm, u_ref, l_ref, lot_ref, uol_ref, iln_ref, iun_ref, ilo_ref, iuo_ref,
    strip_ref, band_ref, small_ref,
    a_ref, ah, al, xu, xl, ut, lt, pb, ps, rb, rp, bc, part, r1, s2, r2, ag, uni, lni,
    asem, rs_send, rs_recv, cs_send, cs_recv,
):
    r, c = lax.axis_index("row"), lax.axis_index("col")
    rows, cols = a_hbm.shape
    wu, wl = cols // nr, rows // nc
    width = iln_ref.shape[0]
    hu, hl = width // nr, width // nc
    load = pltpu.make_async_copy(a_hbm, a_ref, asem)
    load.start()
    barrier = pltpu.get_barrier_semaphore()
    for d in range(1, nr):
        pl.semaphore_signal(barrier, inc=1, device_id={"row": lax.rem(r + d, nr)}, device_id_type=pl.DeviceIdType.MESH)
    for d in range(1, nc):
        pl.semaphore_signal(barrier, inc=1, device_id={"col": lax.rem(c + d, nc)}, device_id_type=pl.DeviceIdType.MESH)
    pl.semaphore_wait(barrier, nr + nc - 2)

    def ucol(i):
        return pl.ds(pl.multiple_of(i * wu, wu), wu)

    def lcol(i):
        return pl.ds(pl.multiple_of(i * wl, wl), wl)

    def row_stage(k, source, target):
        return start("row", nr, r, source, target, rs_send.at[k], rs_recv.at[k])

    def col_stage(k, source, target):
        return start("col", nc, c, source, target, cs_send.at[k], cs_recv.at[k])

    every = []
    u0 = row_stage(0, lambda p: u_ref.at[:, ucol(p)], xu.at[r])
    l0 = col_stage(0, lambda p: l_ref.at[:, lcol(p)], xl.at[c])
    xu[r] = u_ref[:, ucol(r)]
    xl[c] = l_ref[:, lcol(c)]
    iun, iuo = split(iun_ref[...]), split(iuo_ref[...])
    mix_u = split(mul(split(mul(iuo, split(uol_ref[...]))), iun))
    ilo = ilo_ref[...]
    mix_l = mul(split(mul(split(iln_ref[...]), split(lot_ref[...]))), split(ilo))
    mix_l, ilo, iln = split(mix_l.T), split(ilo.T), split(iln_ref[...].T)
    arrive(u0)
    un = split(xu[:, :hu].reshape(width, wu))
    ut[:, ucol(r)] = mul(iuo, split(xu[:, hu:].reshape(width, wu))) - mul(mix_u, un)
    u1 = row_stage(1, lambda p: ut.at[:, ucol(r)], ut.at[:, ucol(r)])
    arrive(l0)
    ln = split(xl[:, :hl].reshape(width, wl))
    lt[:, lcol(c)] = mul(ilo, split(xl[:, hl:].reshape(width, wl))) - mul(mix_l, ln)
    l1 = col_stage(1, lambda p: lt.at[:, lcol(c)], lt.at[:, lcol(c)])
    uni[...] = mul(iun, un)
    lni[...] = mul(iln, ln)
    load.wait()
    high, low = split(a_ref[...])
    ah[...] = high
    al[...] = low
    arrive(l1)
    lts = split(lt[...])
    tile = 2 * wu
    for i in range(cols // tile):
        here = slice(i * tile, (i + 1) * tile)
        pb[:, here] = -mul(lts, (ah[:, here], al[:, here]))
    b0 = row_stage(2, lambda p: pb.at[:, ucol(p)], rb.at[r])
    rb[r] = pb[:, ucol(r)]
    arrive(u1)
    uts = split(ut[...])
    tile = 2 * wl
    for i in range(rows // tile):
        here = slice(i * tile, (i + 1) * tile)
        ps[here] = -mul((ah[here], al[here]), uts, NT)
    p0 = col_stage(2, lambda p: ps.at[lcol(p)], rp.at[c])
    rp[c] = ps[lcol(c)]
    arrive(b0)
    band = rb[0]
    for i in range(1, nr):
        band = band + rb[i]
    bc[...] = band
    arrive(p0)
    strip = rp[0]
    for i in range(1, nc):
        strip = strip + rp[i]
    strip_ref[...] = strip
    b1 = row_stage(3, lambda p: bc, band_ref.at[:, ucol(r)])
    band_ref[:, ucol(r)] = band
    part[:width] = -mul(split(band), split(uni[...]), NT)
    strip = split(strip)
    part[width : 2 * width] = -mul(split(lni[...]), strip)
    part[2 * width :] = -mul(split(lt[:, lcol(c)]), strip)
    high = 3 * width // nc
    each = high // nr
    s0 = col_stage(3, lambda p: part.at[pl.ds(pl.multiple_of(p * high, high), high)], r1.at[c])
    r1[c] = part[pl.ds(pl.multiple_of(c * high, high), high)]
    arrive(s0)
    total = r1[0]
    for i in range(1, nc):
        total = total + r1[i]
    for i in range(nr):
        s2[i] = total[i * each : (i + 1) * each]
    s1 = row_stage(4, lambda p: s2.at[p], r2.at[r])
    r2[r] = s2[r]
    arrive(s1)
    total = r2[0]
    for i in range(1, nr):
        total = total + r2[i]
    ag[r] = total
    s3 = row_stage(5, lambda p: ag.at[r], ag.at[r])
    arrive(s3)
    s4 = col_stage(4, lambda p: ag, small_ref.at[c])
    small_ref[c] = ag[...]
    arrive(s4)
    arrive(b1)
    for group in (u0, l0, u1, l1, b0, p0, b1, s0, s1, s3, s4):
        for copy in group:
            copy.wait_send()


def body(an, ln, un, lot, lo, uol, uo, dln, dun, iln, iun, dlo, duo, ilo, iuo):
    nr, nc = lax.axis_size("row"), lax.axis_size("col")
    rows, cols = an.shape
    width = iln.shape[0]
    wu, wl = cols // nr, rows // nc
    u = jnp.concatenate((un, uo), axis=0)
    l = jnp.concatenate((ln, lo), axis=1).T
    high = 3 * width // nc
    each = high // nr
    vm = pl.BlockSpec(memory_space=pltpu.VMEM)
    V = pltpu.VMEM
    strip, band, small = pl.pallas_call(
        functools.partial(kernel, nr, nc),
        out_shape=(
            jax.ShapeDtypeStruct((wl, width), f32),
            jax.ShapeDtypeStruct((width, cols), f32),
            jax.ShapeDtypeStruct((nc, nr, each, width), f32),
        ),
        in_specs=[pl.BlockSpec(memory_space=pl.ANY)] + [vm] * 8,
        out_specs=(vm, vm, vm),
        scratch_shapes=[
            V((rows, cols), f32), V((rows, cols), bf16), V((rows, cols), bf16),
            V((nr, 2 * width // nr, wu), f32), V((nc, 2 * width // nc, wl), f32),
            V((width, cols), f32), V((width, rows), f32),
            V((width, cols), f32), V((rows, width), f32),
            V((nr, width, wu), f32), V((nc, wl, width), f32),
            V((width, wu), f32), V((3 * width, width), f32),
            V((nc, high, width), f32), V((nr, each, width), f32),
            V((nr, each, width), f32), V((nr, each, width), f32),
            V((width, wu), f32), V((width, wl), f32),
            pltpu.SemaphoreType.DMA,
            pltpu.SemaphoreType.DMA((6, nr)), pltpu.SemaphoreType.DMA((6, nr)),
            pltpu.SemaphoreType.DMA((5, nc)), pltpu.SemaphoreType.DMA((5, nc)),
        ],
        compiler_params=pltpu.CompilerParams(collective_id=0, has_side_effects=True),
    )(an, u, l, lot, uol, iln, iun, ilo, iuo)
    small = small.reshape(3 * width, width)
    return small[2 * width :], small[width : 2 * width], strip, small[:width], band


def solution(mesh):
    two, whole = P("row", "col"), P()
    return jax.shard_map(
        body,
        mesh=mesh,
        in_specs=(two, two, two, whole, two, whole, two) + (whole,) * 8,
        out_specs=(P(), P(), P(("row", "col"), None), P(), P(None, "col")),
        check_vma=False,
    )
```

```python
import functools

import jax
import jax.numpy as jnp
from jax import lax
from jax.experimental import pallas as pl
from jax.experimental.pallas import tpu as pltpu
from jax.sharding import PartitionSpec as P

f32, bf16 = jnp.float32, jnp.bfloat16
NN, NT = ((1,), (0,)), ((1,), (1,))


def split(x):
    high = x.astype(bf16)
    return high, (x - high.astype(f32)).astype(bf16)


def mul(a, b, dims=NN):
    def one(x, y):
        return lax.dot_general(x, y, (dims, ((), ())), preferred_element_type=f32)

    return one(a[0], b[0]) + (one(a[0], b[1]) + one(a[1], b[0]))


def start(axis, n, me, source, target, send, recv):
    copies = []
    for d in range(1, n):
        peer = lax.rem(me + d, n)
        copy = pltpu.make_async_remote_copy(
            src_ref=source(peer),
            dst_ref=target,
            send_sem=send.at[d],
            recv_sem=recv.at[d],
            device_id={axis: peer},
            device_id_type=pl.DeviceIdType.MESH,
        )
        copy.start()
        copies.append(copy)
    return copies


def arrive(copies):
    for copy in copies:
        copy.wait_recv()


def kernel(
    nr, nc, ny, a_hbm, u_ref, l_ref, lot_ref, uol_ref, iln_ref, iun_ref, ilo_ref, iuo_ref,
    strip_ref, band_ref, both_ref, left_ref,
    a_ref, ah, al, xu, xl, ut, lt, pb, ps, ry, sz, rz, rp, bc, uni, lni,
    pa, ra, sa, ta, ga, pl_, rl, sl, tl, gl,
    asem, rs_send, rs_recv, cs_send, cs_recv,
):
    r, c = lax.axis_index("row"), lax.axis_index("col")
    rows, cols = a_hbm.shape
    wu, wl = cols // nr, rows // nc
    width = iln_ref.shape[0]
    hu, hl = width // nr, width // nc
    nz = nr // ny
    z, y = r // ny, lax.rem(r, ny)
    far = [nz // 2] * (nz > 1) + [k for k in range(nz - 1, 0, -1) if k != nz // 2]
    load = pltpu.make_async_copy(a_hbm, a_ref, asem)
    load.start()
    barrier = pltpu.get_barrier_semaphore()
    for d in range(1, nr):
        pl.semaphore_signal(barrier, inc=1, device_id={"row": lax.rem(r + d, nr)}, device_id_type=pl.DeviceIdType.MESH)
    for d in range(1, nc):
        pl.semaphore_signal(barrier, inc=1, device_id={"col": lax.rem(c + d, nc)}, device_id_type=pl.DeviceIdType.MESH)
    pl.semaphore_wait(barrier, nr + nc - 2)

    def ucol(i):
        return pl.ds(pl.multiple_of(i * wu, wu), wu)

    def lcol(i):
        return pl.ds(pl.multiple_of(i * wl, wl), wl)

    sent = []

    def row_stage(k, source, target):
        copies = start("row", nr, r, source, target, rs_send.at[k], rs_recv.at[k])
        sent.extend(copies)
        return copies

    def col_stage(k, source, target):
        copies = start("col", nc, c, source, target, cs_send.at[k], cs_recv.at[k])
        sent.extend(copies)
        return copies

    def push(stage, index, source, target, zi, yi):
        copy = pltpu.make_async_remote_copy(
            src_ref=source,
            dst_ref=target,
            send_sem=rs_send.at[stage, index],
            recv_sem=rs_recv.at[stage, index],
            device_id={"row": zi * ny + yi},
            device_id_type=pl.DeviceIdType.MESH,
        )
        copy.start()
        sent.append(copy)
        return copy

    def across(stage, k, source, slot):
        return [push(stage, k * ny + d, source, slot, z, lax.rem(y + d, ny)) for d in range(1, ny)]

    def gather_start(stage, source, slot):
        along = {k: push(stage, k, source, slot(r), lax.rem(z + k, nz), y) for k in far}
        return along, across(stage + 1, 0, source, slot(r))

    def gather_pass(stage, state, slot):
        along, over = state
        for k in far[::-1]:
            along[k].wait_recv()
            here = slot(lax.rem(z - k + nz, nz) * ny + y)
            over.extend(across(stage + 1, k, here, here))
        return over

    u0 = row_stage(0, lambda p: u_ref.at[:, ucol(p)], xu.at[r])
    l0 = col_stage(0, lambda p: l_ref.at[:, lcol(p)], xl.at[c])
    xu[r] = u_ref[:, ucol(r)]
    xl[c] = l_ref[:, lcol(c)]
    iun, iuo = split(iun_ref[...]), split(iuo_ref[...])
    mix_u = split(mul(split(mul(iuo, split(uol_ref[...]))), iun))
    ilo = ilo_ref[...]
    mix_l = mul(split(mul(split(iln_ref[...]), split(lot_ref[...]))), split(ilo))
    mix_l, ilo, iln = split(mix_l.T), split(ilo.T), split(iln_ref[...].T)
    arrive(u0)
    un = split(xu[:, :hu].reshape(width, wu))
    ut[:, ucol(r)] = mul(iuo, split(xu[:, hu:].reshape(width, wu))) - mul(mix_u, un)
    uslot = lambda i: ut.at[:, ucol(i)]
    u1 = gather_start(1, uslot(r), uslot)
    arrive(l0)
    ln = split(xl[:, :hl].reshape(width, wl))
    lt[:, lcol(c)] = mul(ilo, split(xl[:, hl:].reshape(width, wl))) - mul(mix_l, ln)
    l1 = col_stage(1, lambda p: lt.at[:, lcol(c)], lt.at[:, lcol(c)])
    uni[...] = mul(iun, un)
    lni[...] = mul(iln, ln)
    load.wait()
    high, low = split(a_ref[...])
    ah[...] = high
    al[...] = low
    arrive(l1)
    lts = split(lt[...])
    tile = 2 * wu
    for i in range(cols // tile):
        here = slice(i * tile, (i + 1) * tile)
        pb[:, here] = -mul(lts, (ah[:, here], al[:, here]))
    b0 = {}
    for k in far + [0]:
        zt = lax.rem(z + k, nz)
        b0[k] = [
            push(3, k * ny + d, pb.at[:, ucol(zt * ny + lax.rem(y + d, ny))], ry.at[k, d], z, lax.rem(y + d, ny))
            for d in range(1, ny)
        ]
    over = gather_pass(1, u1, uslot)
    b1 = {}
    for k in far + [0]:
        arrive(b0[k])
        zt = lax.rem(z + k, nz)
        total = pb[:, ucol(zt * ny + y)]
        for d in range(1, ny):
            total = total + ry[k, d]
        if k:
            sz[k] = total
            b1[k] = push(4, k, sz.at[k], rz.at[k], zt, y)
        else:
            rz[0] = total
    arrive(over)
    uts = split(ut[...])
    tile = 2 * wl
    for i in range(rows // tile):
        here = slice(i * tile, (i + 1) * tile)
        ps[here] = -mul((ah[here], al[here]), uts, NT)
    p0 = col_stage(2, lambda p: ps.at[lcol(p)], rp.at[c])
    rp[c] = ps[lcol(c)]

    def small_cols(stage, part, got):
        high = part.shape[0] // nc
        at = lambda p: part.at[pl.ds(pl.multiple_of(p * high, high), high)]
        copies = col_stage(stage, at, got.at[c])
        got[c] = part[pl.ds(pl.multiple_of(c * high, high), high)]
        return copies

    def small_rows(stage, copies, got, send, take):
        arrive(copies)
        total = got[0]
        for i in range(1, nc):
            total = total + got[i]
        each = send.shape[1]
        for i in range(nr):
            send[i] = total[i * each : (i + 1) * each]
        copies = row_stage(stage, lambda p: send.at[p], take.at[r])
        take[r] = send[r]
        return copies

    def back_rows(stage, copies, take, whole):
        arrive(copies)
        total = take[0]
        for i in range(1, nr):
            total = total + take[i]
        whole[r] = total
        return row_stage(stage, lambda p: whole.at[r], whole.at[r])

    def back_cols(stage, copies, whole, out):
        arrive(copies)
        copies = col_stage(stage, lambda p: whole, out.at[c])
        out[c] = whole[...]
        return copies

    arrive([b1[k] for k in far])
    band = rz[0]
    for k in range(1, nz):
        band = band + rz[k]
    bc[...] = band
    bslot = lambda i: band_ref.at[:, ucol(i)]
    b2 = gather_start(5, bc, bslot)
    band_ref[:, ucol(r)] = band
    pl_[...] = -mul(split(band), split(uni[...]), NT)
    left = small_cols(3, pl_, rl)
    arrive(p0)
    strip = rp[0]
    for i in range(1, nc):
        strip = strip + rp[i]
    strip_ref[...] = strip
    strip = split(strip)
    pa[:width] = -mul(split(lni[...]), strip)
    pa[width:] = -mul(split(lt[:, lcol(c)]), strip)
    both = small_cols(4, pa, ra)
    left = small_rows(7, left, rl, sl, tl)
    both = small_rows(8, both, ra, sa, ta)
    left = back_rows(9, left, tl, gl)
    both = back_rows(10, both, ta, ga)
    left = back_cols(5, left, gl, left_ref)
    both = back_cols(6, both, ga, both_ref)
    over = gather_pass(5, b2, bslot)
    arrive(left)
    arrive(both)
    arrive(over)
    for copy in sent:
        copy.wait_send()


def body(an, ln, un, lot, lo, uol, uo, dln, dun, iln, iun, dlo, duo, ilo, iuo):
    nr, nc = lax.axis_size("row"), lax.axis_size("col")
    rows, cols = an.shape
    width = iln.shape[0]
    wu, wl = cols // nr, rows // nc
    u = jnp.concatenate((un, uo), axis=0)
    l = jnp.concatenate((ln, lo), axis=1).T
    ny = nc // 2 if nc % 2 == 0 and nr % max(nc // 2, 1) == 0 else 1
    nz = nr // ny
    vm = pl.BlockSpec(memory_space=pltpu.VMEM)
    V = pltpu.VMEM

    def chain(size):
        high = size // nc
        whole = V((nr, high // nr, width), f32)
        return [V((size, width), f32), V((nc, high, width), f32), whole, whole, whole]

    D = pltpu.SemaphoreType.DMA
    strip, band, both, left = pl.pallas_call(
        functools.partial(kernel, nr, nc, ny),
        out_shape=(
            jax.ShapeDtypeStruct((wl, width), f32),
            jax.ShapeDtypeStruct((width, cols), f32),
            jax.ShapeDtypeStruct((nc, nr, 2 * width // nc // nr, width), f32),
            jax.ShapeDtypeStruct((nc, nr, width // nc // nr, width), f32),
        ),
        in_specs=[pl.BlockSpec(memory_space=pl.ANY)] + [vm] * 8,
        out_specs=(vm, vm, vm, vm),
        scratch_shapes=[
            V((rows, cols), f32), V((rows, cols), bf16), V((rows, cols), bf16),
            V((nr, 2 * width // nr, wu), f32), V((nc, 2 * width // nc, wl), f32),
            V((width, cols), f32), V((width, rows), f32),
            V((width, cols), f32), V((rows, width), f32),
            V((nz, ny, width, wu), f32), V((nz, width, wu), f32), V((nz, width, wu), f32),
            V((nc, wl, width), f32), V((width, wu), f32),
            V((width, wu), f32), V((width, wl), f32),
            *chain(2 * width), *chain(width),
            D, D((11, nr)), D((11, nr)), D((7, nc)), D((7, nc)),
        ],
        compiler_params=pltpu.CompilerParams(collective_id=0, has_side_effects=True),
    )(an, u, l, lot, uol, iln, iun, ilo, iuo)
    both = both.reshape(2 * width, width)
    return both[width:], both[:width], strip, left.reshape(width, width), band


def solution(mesh):
    two, whole = P("row", "col"), P()
    return jax.shard_map(
        body,
        mesh=mesh,
        in_specs=(two, two, two, whole, two, whole, two) + (whole,) * 8,
        out_specs=(P(), P(), P(("row", "col"), None), P(), P(None, "col")),
        check_vma=False,
    )
```

```python
import functools

import jax
import jax.numpy as jnp
from jax import lax
from jax.experimental import pallas as pl
from jax.experimental.pallas import tpu as pltpu
from jax.sharding import PartitionSpec as P

f32, bf16 = jnp.float32, jnp.bfloat16
NN, NT = ((1,), (0,)), ((1,), (1,))


def split(x):
    high = x.astype(bf16)
    return high, (x - high.astype(f32)).astype(bf16)


def mul(a, b, dims=NN):
    def one(x, y):
        return lax.dot_general(x, y, (dims, ((), ())), preferred_element_type=f32)

    return one(a[0], b[0]) + (one(a[0], b[1]) + one(a[1], b[0]))


def start(axis, n, me, source, target, send, recv):
    copies = []
    for d in range(1, n):
        peer = lax.rem(me + d, n)
        copy = pltpu.make_async_remote_copy(
            src_ref=source(peer),
            dst_ref=target,
            send_sem=send.at[d],
            recv_sem=recv.at[d],
            device_id={axis: peer},
            device_id_type=pl.DeviceIdType.MESH,
        )
        copy.start()
        copies.append(copy)
    return copies


def arrive(copies):
    for copy in copies:
        copy.wait_recv()


def kernel(
    nr, nc, ny, a_hbm, un_ref, uo_ref, l_ref, lot_hbm, uol_hbm, iln_hbm, iun_hbm, ilo_hbm, iuo_hbm,
    strip_ref, band_ref, both_ref, left_ref,
    a_ref, ah, al, xu, xl, ut, lt, pb, ps, ry, sz, rz, rp, bc, uni, lni,
    pa, ra, sa, ta, ga, pl_, rl, sl, tl, gl,
    sq, asem, qsem, rs_send, rs_recv, cs_send, cs_recv,
):
    r, c = lax.axis_index("row"), lax.axis_index("col")
    rows, cols = a_hbm.shape
    wu, wl = cols // nr, rows // nc
    width = iln_hbm.shape[0]
    hl = width // nc
    nz = nr // ny
    z, y = r // ny, lax.rem(r, ny)
    far = [nz // 2] * (nz > 1) + [k for k in range(nz - 1, 0, -1) if k != nz // 2]
    load = pltpu.make_async_copy(a_hbm, a_ref, asem)
    squares = (iuo_hbm, uol_hbm, iun_hbm, iln_hbm, lot_hbm, ilo_hbm)
    loads = [pltpu.make_async_copy(m, sq.at[i], qsem.at[i]) for i, m in enumerate(squares)]
    for copy in loads:
        copy.start()
    load.start()
    barrier = pltpu.get_barrier_semaphore()
    for d in range(1, nr):
        pl.semaphore_signal(barrier, inc=1, device_id={"row": lax.rem(r + d, nr)}, device_id_type=pl.DeviceIdType.MESH)
    for d in range(1, nc):
        pl.semaphore_signal(barrier, inc=1, device_id={"col": lax.rem(c + d, nc)}, device_id_type=pl.DeviceIdType.MESH)
    pl.semaphore_wait(barrier, nr + nc - 2)

    def ucol(i):
        return pl.ds(pl.multiple_of(i * wu, wu), wu)

    def lcol(i):
        return pl.ds(pl.multiple_of(i * wl, wl), wl)

    sent = []

    def row_stage(k, source, target):
        copies = start("row", nr, r, source, target, rs_send.at[k], rs_recv.at[k])
        sent.extend(copies)
        return copies

    def col_stage(k, source, target):
        copies = start("col", nc, c, source, target, cs_send.at[k], cs_recv.at[k])
        sent.extend(copies)
        return copies

    def push(stage, index, source, target, zi, yi):
        copy = pltpu.make_async_remote_copy(
            src_ref=source,
            dst_ref=target,
            send_sem=rs_send.at[stage, index],
            recv_sem=rs_recv.at[stage, index],
            device_id={"row": zi * ny + yi},
            device_id_type=pl.DeviceIdType.MESH,
        )
        copy.start()
        sent.append(copy)
        return copy

    def across(stage, k, source, slot):
        return [push(stage, k * ny + d, source, slot, z, lax.rem(y + d, ny)) for d in range(1, ny)]

    def gather_start(stage, source, slot):
        along = {k: push(stage, k, source, slot(r), lax.rem(z + k, nz), y) for k in far}
        return along, across(stage + 1, 0, source, slot(r))

    def gather_pass(stage, state, slot):
        along, over = state
        for k in far[::-1]:
            along[k].wait_recv()
            here = slot(lax.rem(z - k + nz, nz) * ny + y)
            over.extend(across(stage + 1, k, here, here))
        return over

    u0 = row_stage(0, lambda p: un_ref.at[:, ucol(p)], xu.at[0, r])
    u0 = u0 + row_stage(11, lambda p: uo_ref.at[:, ucol(p)], xu.at[1, r])
    l0 = col_stage(0, lambda p: l_ref.at[:, lcol(p)], xl.at[c])
    xu[0, r] = un_ref[:, ucol(r)]
    xu[1, r] = uo_ref[:, ucol(r)]
    xl[c] = l_ref[:, lcol(c)]
    for copy in loads:
        copy.wait()
    iuo, iun = split(sq[0]), split(sq[2])
    mix_u = split(mul(split(mul(iuo, split(sq[1]))), iun))
    ilo = sq[5]
    mix_l = mul(split(mul(split(sq[3]), split(sq[4]))), split(ilo))
    mix_l, ilo, iln = split(mix_l.T), split(ilo.T), split(sq[3].T)
    arrive(u0)
    un = split(xu[0].reshape(width, wu))
    ut[:, ucol(r)] = mul(iuo, split(xu[1].reshape(width, wu))) - mul(mix_u, un)
    uslot = lambda i: ut.at[:, ucol(i)]
    u1 = gather_start(1, uslot(r), uslot)
    arrive(l0)
    ln = split(xl[:, :hl].reshape(width, wl))
    lt[:, lcol(c)] = mul(ilo, split(xl[:, hl:].reshape(width, wl))) - mul(mix_l, ln)
    l1 = col_stage(1, lambda p: lt.at[:, lcol(c)], lt.at[:, lcol(c)])
    uni[...] = mul(iun, un)
    lni[...] = mul(iln, ln)
    load.wait()
    high, low = split(a_ref[...])
    ah[...] = high
    al[...] = low
    arrive(l1)
    lts = split(lt[...])
    tile = 2 * wu
    for i in range(cols // tile):
        here = slice(i * tile, (i + 1) * tile)
        pb[:, here] = -mul(lts, (ah[:, here], al[:, here]))
    b0 = {}
    for k in far + [0]:
        zt = lax.rem(z + k, nz)
        b0[k] = [
            push(3, k * ny + d, pb.at[:, ucol(zt * ny + lax.rem(y + d, ny))], ry.at[k, d], z, lax.rem(y + d, ny))
            for d in range(1, ny)
        ]
    over = gather_pass(1, u1, uslot)
    b1 = {}
    for k in far + [0]:
        arrive(b0[k])
        zt = lax.rem(z + k, nz)
        total = pb[:, ucol(zt * ny + y)]
        for d in range(1, ny):
            total = total + ry[k, d]
        if k:
            sz[k] = total
            b1[k] = push(4, k, sz.at[k], rz.at[k], zt, y)
        else:
            rz[0] = total
    arrive(over)
    uts = split(ut[...])
    tile = 2 * wl
    for i in range(rows // tile):
        here = slice(i * tile, (i + 1) * tile)
        ps[here] = -mul((ah[here], al[here]), uts, NT)
    p0 = col_stage(2, lambda p: ps.at[lcol(p)], rp.at[c])
    rp[c] = ps[lcol(c)]

    def small_cols(stage, part, got):
        high = part.shape[0] // nc
        at = lambda p: part.at[pl.ds(pl.multiple_of(p * high, high), high)]
        copies = col_stage(stage, at, got.at[c])
        got[c] = part[pl.ds(pl.multiple_of(c * high, high), high)]
        return copies

    def small_rows(stage, copies, got, send, take):
        arrive(copies)
        total = got[0]
        for i in range(1, nc):
            total = total + got[i]
        each = send.shape[1]
        for i in range(nr):
            send[i] = total[i * each : (i + 1) * each]
        copies = row_stage(stage, lambda p: send.at[p], take.at[r])
        take[r] = send[r]
        return copies

    def back_rows(stage, copies, take, whole):
        arrive(copies)
        total = take[0]
        for i in range(1, nr):
            total = total + take[i]
        whole[r] = total
        return row_stage(stage, lambda p: whole.at[r], whole.at[r])

    def back_cols(stage, copies, whole, out):
        arrive(copies)
        copies = col_stage(stage, lambda p: whole, out.at[c])
        out[c] = whole[...]
        return copies

    arrive([b1[k] for k in far])
    band = rz[0]
    for k in range(1, nz):
        band = band + rz[k]
    bc[...] = band
    bslot = lambda i: band_ref.at[:, ucol(i)]
    b2 = gather_start(5, bc, bslot)
    band_ref[:, ucol(r)] = band
    pl_[...] = -mul(split(band), split(uni[...]), NT)
    left = small_cols(3, pl_, rl)
    arrive(p0)
    strip = rp[0]
    for i in range(1, nc):
        strip = strip + rp[i]
    strip_ref[...] = strip
    strip = split(strip)
    pa[:width] = -mul(split(lni[...]), strip)
    pa[width:] = -mul(split(lt[:, lcol(c)]), strip)
    both = small_cols(4, pa, ra)
    left = small_rows(7, left, rl, sl, tl)
    both = small_rows(8, both, ra, sa, ta)
    over = gather_pass(5, b2, bslot)
    left = back_rows(9, left, tl, gl)
    both = back_rows(10, both, ta, ga)
    left = back_cols(5, left, gl, left_ref)
    both = back_cols(6, both, ga, both_ref)
    arrive(left)
    arrive(both)
    arrive(over)
    for copy in sent:
        copy.wait_send()


def body(an, ln, un, lot, lo, uol, uo, dln, dun, iln, iun, dlo, duo, ilo, iuo):
    nr, nc = lax.axis_size("row"), lax.axis_size("col")
    rows, cols = an.shape
    width = iln.shape[0]
    wu, wl = cols // nr, rows // nc
    l = jnp.concatenate((ln, lo), axis=1).T
    ny = nc // 2 if nc % 2 == 0 and nr % max(nc // 2, 1) == 0 else 1
    nz = nr // ny
    vm = pl.BlockSpec(memory_space=pltpu.VMEM)
    hbm = pl.BlockSpec(memory_space=pl.ANY)
    V = pltpu.VMEM

    def chain(size):
        high = size // nc
        whole = V((nr, high // nr, width), f32)
        return [V((size, width), f32), V((nc, high, width), f32), whole, whole, whole]

    D = pltpu.SemaphoreType.DMA
    strip, band, both, left = pl.pallas_call(
        functools.partial(kernel, nr, nc, ny),
        out_shape=(
            jax.ShapeDtypeStruct((wl, width), f32),
            jax.ShapeDtypeStruct((width, cols), f32),
            jax.ShapeDtypeStruct((nc, nr, 2 * width // nc // nr, width), f32),
            jax.ShapeDtypeStruct((nc, nr, width // nc // nr, width), f32),
        ),
        in_specs=[hbm, vm, vm, vm] + [hbm] * 6,
        out_specs=(vm, vm, vm, vm),
        scratch_shapes=[
            V((rows, cols), f32), V((rows, cols), bf16), V((rows, cols), bf16),
            V((2, nr, width // nr, wu), f32), V((nc, 2 * width // nc, wl), f32),
            V((width, cols), f32), V((width, rows), f32),
            V((width, cols), f32), V((rows, width), f32),
            V((nz, ny, width, wu), f32), V((nz, width, wu), f32), V((nz, width, wu), f32),
            V((nc, wl, width), f32), V((width, wu), f32),
            V((width, wu), f32), V((width, wl), f32),
            *chain(2 * width), *chain(width),
            V((6, width, width), f32), D, D((6,)), D((12, nr)), D((12, nr)), D((7, nc)), D((7, nc)),
        ],
        compiler_params=pltpu.CompilerParams(collective_id=0, has_side_effects=True),
    )(an, un, uo, l, lot, uol, iln, iun, ilo, iuo)
    both = both.reshape(2 * width, width)
    return both[width:], both[:width], strip, left.reshape(width, width), band


def solution(mesh):
    two, whole = P("row", "col"), P()
    return jax.shard_map(
        body,
        mesh=mesh,
        in_specs=(two, two, two, whole, two, whole, two) + (whole,) * 8,
        out_specs=(P(), P(), P(("row", "col"), None), P(), P(None, "col")),
        check_vma=False,
    )
```
